32 devices in a mesh: beam: 2 (over x), freq: 8 (over z, y), tm: 2 (over core).
Axes of the slice: x: 2, y: 2, z: 4, core: 2. Of those that a mesh axis runs over, the one named last changes fastest.
Arguments:
- spectra: float32 [4096, 5120], P(('beam', 'freq'), 'tm'), parts along dimension 0, may hold values from -6 to 6
- delays: int32 [11, 2048], replicated, may hold values from 0 to 1024, as said below
- widths: int32 [8], replicated, may hold values from 1 to 128, as said below
Outputs:
- filtered: float32 [8, 4096, 5120], P(None, ('beam', 'freq'), 'tm'), parts along dimension 1
The draws below stay inside these ranges and needn't reach their ends.
There are 2 independent parts, one for each index of `beam`. The reference program is written for one: setup_inputs(seed, part) draws one part's arguments, and reference() takes and returns one part's arrays. A program takes and returns all parts, laid end to end along the dimension named above; an argument that names none is the same for every part. Nothing has to cross between parts.
Inputs may be any that keep to these rules, and one draw needn't show every extreme that they name: delays[l, r] lies in 0 to 2 ** l, and every level l has some entry equal to 2 ** l. The widths include 1 and 128.
All inputs are finite; a program needn't handle non-finite values.
Results may differ from the reference program's by a relative error of at most 0.0003.
Values sent between devices are 32-bit elements; how exact they have to be, the bound alone decides.
A program may use at most 192 MiB of HBM per device.

```python
import jax
import jax.numpy as jnp
from jax import lax

F = 2048
LEVELS = 11
NW = 8
TAPS = 128
S = 5120


def draw_delays(key, part):
    draw_key, place_key = jax.random.split(jax.random.fold_in(key, 11))
    bounds = (2 ** jnp.arange(LEVELS)).astype(jnp.int32)
    delay_table = jax.random.randint(draw_key, (LEVELS, F), 0, bounds[:, None] + 1)
    column = jax.random.randint(place_key, (LEVELS,), 0, F)
    delay_table = delay_table.at[jnp.arange(LEVELS), column].set(bounds)
    return delay_table.astype(jnp.int32)


def draw_widths(key, part):
    draw_key, place_key = jax.random.split(jax.random.fold_in(key, 23))
    values = jax.random.randint(draw_key, (NW,), 2, TAPS)
    shuffled = jax.random.permutation(place_key, NW)
    values = values.at[shuffled[0]].set(1).at[shuffled[1]].set(TAPS)
    return values.astype(jnp.int32)


def block_levels(key, dims, cuts, low, high):
    loudness = 1.0
    for position, parts in cuts:
        steps = jax.random.uniform(jax.random.fold_in(jax.random.fold_in(key, 6), position), (parts,), jnp.float32, low / len(cuts), high / len(cuts))
        loudness = loudness * jnp.repeat(jnp.exp(steps), dims[position] // parts).reshape((-1,) + (1,) * (len(dims) - 1 - position))
    return loudness


def noise(own_key, extent, width, bound, cuts=(), kind=jnp.bfloat16):
    level = block_levels(own_key, extent, cuts, -0.22, 0.18) if cuts else 1.0
    drawn = jax.random.normal(own_key, extent, jnp.float32) * width * level
    return jnp.minimum(jnp.maximum(drawn, -bound), bound).astype(kind)


def setup_inputs(seed: int = 0, part: int = 0) -> dict:
    arg_keys = jax.random.split(jax.random.key(seed), 4)
    part_keys = jax.random.split(jax.random.fold_in(arg_keys[3], part), 4)
    return {
        "spectra": noise(part_keys[0], (F, S), 1.0, 6.0, ((0, 8), (1, 2)), jnp.float32),
        "delays": draw_delays(jax.random.fold_in(arg_keys[3], 71), part),
        "widths": draw_widths(jax.random.fold_in(arg_keys[3], 71), part),
    }


def delay_level(current, row_shifts, half_rows):
    row_count, out_width = current.shape
    group_count = row_count // (2 * half_rows)
    block_view = current.reshape(group_count, 2, half_rows, out_width)
    padded = jnp.pad(block_view[:, 1], ((0, 0), (0, 0), (0, half_rows)))
    source_rows = jnp.broadcast_to(padded[:, None], (group_count, 2, half_rows, out_width + half_rows))
    source_rows = source_rows.reshape(row_count, out_width + half_rows)
    delayed = jax.vmap(lambda row_data, offset_at: lax.dynamic_slice_in_dim(row_data, offset_at, out_width))(source_rows, row_shifts.astype(jnp.int32))
    summed = block_view[:, 0][:, None] + delayed.reshape(group_count, 2, half_rows, out_width)
    return summed.reshape(row_count, out_width)

def reference(spectra, delays, widths):
    current = spectra
    for tree_level in range(LEVELS):
        current = delay_level(current, delays[tree_level], 2 ** tree_level)
    padded = jnp.pad(current, ((0, 0), (1, TAPS)))
    running = jnp.cumsum(padded, axis=1)

    def filter_one(box_width):
        upper_sum = lax.dynamic_slice_in_dim(running, box_width.astype(jnp.int32), S, 1)
        scaling = 1.0 / jnp.sqrt(box_width.astype(jnp.float32) * F)
        return (upper_sum - running[:, :S]) * scaling
    return lax.map(filter_one, widths)
```

```python
import functools

import jax
import jax.numpy as jnp
from jax import lax
from jax.experimental import pallas as pl
from jax.experimental.pallas import tpu as pltpu
from jax.sharding import PartitionSpec as P

LANES = 128
SUB = 8
TAPS = 128
VMEM = pltpu.MemorySpace.VMEM
SMEM = pltpu.MemorySpace.SMEM


def cdiv(a, b):
    return -(-a // b)


def lane_shift(low, high, shift, lane):
    picked = jnp.where(lane < shift, high, low)
    return jnp.take_along_axis(
        picked, (lane + shift) & (LANES - 1), axis=1, mode="promise_in_bounds"
    )


def local_tree_kernel(levels, blocks, lead_blocks, own, spectra, lead, shifts, out, buf_a, buf_b):
    rows = spectra.shape[0]
    lane = lax.broadcasted_iota(jnp.int32, (SUB, LANES), 1)
    sub = lax.broadcasted_iota(jnp.int32, (SUB, LANES), 0)

    def out_blocks(level):
        return blocks + cdiv(2**levels - 2 ** (level + 1), LANES)

    def shift_of(group, level):
        col = shifts[pl.ds(group * SUB, SUB), level : level + 1]
        return jnp.broadcast_to(col, (SUB, LANES))

    def first_levels(group, carry):
        at = pl.ds(pl.multiple_of(group * SUB, SUB), SUB)
        x = [spectra[at, b * LANES : (b + 1) * LANES] for b in range(blocks)]
        x += [lead[at, b * LANES : (b + 1) * LANES] for b in range(lead_blocks)]
        for level in range(3):
            h = 2**level
            shift = shift_of(group, level)
            upper = (sub & h) != 0
            b_rows = [jnp.where(upper, v, pltpu.roll(v, SUB - h, 0)) for v in x]
            nxt = []
            for b in range(out_blocks(level)):
                a_rows = jnp.where(upper, pltpu.roll(x[b], h, 0), x[b])
                high = b_rows[min(b + 1, len(x) - 1)]
                nxt.append(a_rows + lane_shift(b_rows[b], high, shift, lane))
            x = nxt
        for b, v in enumerate(x):
            buf_a[b, at, :] = v
        return carry

    lax.fori_loop(0, rows // SUB, first_levels, 0)

    def store(dst, last, b, group, value):
        if not last:
            dst[b, pl.ds(pl.multiple_of(group * SUB, SUB), SUB), :] = value
        elif own % SUB == 0:
            per = own // SUB
            dst[group // per, b, pl.ds(pl.multiple_of((group % per) * SUB, SUB), SUB), :] = value
        else:
            for r in range(SUB):
                dst[group * (SUB // own) + r // own, b, r % own : r % own + 1, :] = value[r : r + 1]

    src, dst = buf_a, buf_b
    for level in range(3, levels):
        last = level == levels - 1
        target = out if last else dst
        hg = 2**level // SUB
        in_count = out_blocks(level - 1)
        count = out_blocks(level)

        def pair(p, carry, src=src, target=target, hg=hg, count=count, in_count=in_count, last=last, level=level):
            g_a = (p // hg) * (2 * hg) + p % hg
            g_b = g_a + hg
            at_a = pl.ds(pl.multiple_of(g_a * SUB, SUB), SUB)
            at_b = pl.ds(pl.multiple_of(g_b * SUB, SUB), SUB)
            s_a, s_b = shift_of(g_a, level), shift_of(g_b, level)
            low = src[0, at_b, :]
            for b in range(count):
                high = src[b + 1, at_b, :] if b + 1 < in_count else low
                a = src[b, at_a, :]
                store(target, last, b, g_a, a + lane_shift(low, high, s_a, lane))
                store(target, last, b, g_b, a + lane_shift(low, high, s_b, lane))
                low = high
            return carry

        lax.fori_loop(0, rows // (2 * SUB), pair, 0)
        src, dst = dst, src


def local_tree(spectra, lead, shifts, parts):
    rows, span = spectra.shape
    levels = rows.bit_length() - 1
    blocks = span // LANES
    lead_blocks = lead.shape[1] // LANES
    own = rows // parts
    spec = pl.BlockSpec(memory_space=VMEM)
    buf = pltpu.VMEM((blocks + lead_blocks, rows, LANES), jnp.float32)
    return pl.pallas_call(
        functools.partial(local_tree_kernel, levels, blocks, lead_blocks, own),
        out_shape=jax.ShapeDtypeStruct((parts, blocks, own, LANES), jnp.float32),
        in_specs=[spec] * 3,
        out_specs=spec,
        scratch_shapes=[buf, buf],
    )(spectra, lead, shifts)


def cross_rows(src, dst, shifts, level, bits, own, first, count, in_pitch, out_pitch, windows, width):
    lane = lax.broadcasted_iota(jnp.int32, (width, LANES), 1)
    bands = 2**bits
    step = 2**level

    def one_row(i, carry):
        for j in range(bands):
            base = (j // (2 * step)) * (2 * step) + j % step
            shift = shifts[(level * bands + j) * own + i]
            block = shift // LANES
            rest = shift % LANES
            for w, (start, out_start) in enumerate(windows):
                a = src[pl.ds((base * in_pitch + start) * own + i, width, stride=own), :]
                b_at = ((base + step) * in_pitch + start + block) * own + i
                low = src[pl.ds(b_at, width, stride=own), :]
                high = src[pl.ds(b_at + own, width, stride=own), :]
                moved = pltpu.roll(jnp.where(lane < rest, high, low), (LANES - rest) % LANES, 1)
                dst[pl.ds((j * out_pitch + out_start) * own + i, width, stride=own), :] = a + moved
        return carry

    lax.fori_loop(first, first + count, one_row, 0)


def cross_kernel(bits, own, blocks, halves, pitch, shifts, arrived, out, buf_a, buf_b, sem):
    total = blocks * halves
    bands = 2**bits
    copies = []
    for s in range(bands):
        c = pltpu.make_async_copy(
            arrived.at[pl.ds(s * total * own, total * own), :],
            buf_a.at[pl.ds(s * pitch * own, total * own), :],
            sem.at[s],
        )
        c.start()
        copies.append(c)
    zero = jnp.zeros(((pitch - total) * own, LANES), jnp.float32)
    for s in range(bands):
        for buf in (buf_a, buf_b):
            buf[pl.ds((s * pitch + total) * own, (pitch - total) * own), :] = zero
    for c in copies:
        c.wait()
    src, dst = buf_a, buf_b
    for level in range(bits):
        if level < bits - 1:
            cross_rows(src, dst, shifts, level, bits, own, 0, own, pitch, pitch, [(0, 0)], total)
        else:
            out_blocks = blocks + 1
            windows = [(c * blocks, c * out_blocks) for c in range(halves)]
            cross_rows(src, out, shifts, level, bits, own, 0, own, pitch, halves * out_blocks, windows, out_blocks)
        src, dst = dst, src


def cross_tree(arrived, shifts, bits, own, blocks, halves, reach):
    bands = 2**bits
    pitch = blocks * halves + cdiv(reach, LANES) + 2
    buf = pltpu.VMEM((bands * pitch * own, LANES), jnp.float32)
    return pl.pallas_call(
        functools.partial(cross_kernel, bits, own, blocks, halves, pitch),
        out_shape=jax.ShapeDtypeStruct((bands * halves * (blocks + 1) * own, LANES), jnp.float32),
        in_specs=[pl.BlockSpec(memory_space=SMEM), pl.BlockSpec(memory_space=pl.ANY)],
        out_specs=pl.BlockSpec(memory_space=VMEM),
        scratch_shapes=[buf, buf, pltpu.SemaphoreType.DMA((bands,))],
    )(shifts, arrived)


def filter_kernel(per_step, widths, scaling, x, out, matrix):
    filters, rows, _ = out.shape

    @pl.when(pl.program_id(0) == 0)
    def _():
        pos = lax.broadcasted_iota(jnp.int32, (2 * TAPS, TAPS), 0)
        dist = pos - lax.broadcasted_iota(jnp.int32, (2 * TAPS, TAPS), 1)
        for w in range(filters):
            box = (dist >= 0) & (dist < widths[w])
            matrix[:, w * TAPS : (w + 1) * TAPS] = jnp.where(box, 1.0, 0.0).astype(jnp.bfloat16)

    first = pl.program_id(0) * per_step
    for k in range(per_step):
        b = first + k
        parts = [x[:, b + n, :, :].reshape(rows, LANES) for n in range(2)]
        rows_in = jnp.concatenate(parts, axis=1)
        head = rows_in.astype(jnp.bfloat16)
        tail = (rows_in - head.astype(jnp.float32)).astype(jnp.bfloat16)
        for w in range(filters):
            m = matrix[:, w * TAPS : (w + 1) * TAPS]
            y = jnp.dot(head, m, preferred_element_type=jnp.float32)
            y += jnp.dot(tail, m, preferred_element_type=jnp.float32)
            out[w, :, k * LANES : (k + 1) * LANES] = y * scaling[w]


def filter_rows(x, widths, scaling, rows):
    filters = widths.shape[0]
    blocks = x.shape[1] - 1
    per_step = 2 if blocks % 2 == 0 else 1
    if x.shape[2] % SUB:
        x = jnp.transpose(x, (1, 0, 2, 3)).reshape(1, blocks + 1, rows, LANES)
    return pl.pallas_call(
        functools.partial(filter_kernel, per_step),
        grid=(blocks // per_step,),
        out_shape=jax.ShapeDtypeStruct((filters, rows, blocks * LANES), jnp.float32),
        in_specs=[
            pl.BlockSpec(memory_space=SMEM),
            pl.BlockSpec(memory_space=SMEM),
            pl.BlockSpec(memory_space=VMEM),
        ],
        out_specs=pl.BlockSpec((filters, rows, per_step * LANES), lambda s: (0, 0, s)),
        scratch_shapes=[pltpu.VMEM((2 * TAPS, filters * TAPS), jnp.bfloat16)],
    )(widths, scaling, x)


def local(spectra, delays, widths):
    rows, span = spectra.shape
    all_levels, all_rows = delays.shape
    levels = rows.bit_length() - 1
    bits = all_levels - levels
    bands, halves = lax.axis_size("freq"), lax.axis_size("tm")
    parts = bands * halves
    own = rows // parts
    blocks = span // LANES
    lead_width = cdiv(rows - 1, LANES) * LANES
    position = lax.axis_index("freq")
    lead = lax.ppermute(spectra[:, :lead_width], "tm", [(k, k - 1) for k in range(1, halves)])
    own_shifts = lax.dynamic_slice_in_dim(delays[:levels], position * rows, rows, 1).T
    x = local_tree(spectra, lead, own_shifts, parts)
    x = lax.all_to_all(x, ("freq", "tm"), 0, 0, tiled=True)
    mine = (position * halves + lax.axis_index("tm")) * own
    shifts = lax.dynamic_slice_in_dim(delays[levels:].reshape(bits, bands, rows), mine, own, 2)
    x = cross_tree(
        x.reshape(-1, LANES), shifts.reshape(-1), bits, own, blocks, halves, 2 ** (all_levels - 1)
    )
    x = x.reshape(parts, blocks + 1, own, LANES)
    x = lax.all_to_all(x, ("freq", "tm"), 0, 0, tiled=True)
    scaling = 1.0 / jnp.sqrt(widths.astype(jnp.float32) * all_rows)
    return filter_rows(x, widths, scaling, rows)


def solution(mesh):
    return jax.shard_map(
        local,
        mesh=mesh,
        in_specs=(P(("beam", "freq"), "tm"), P(), P()),
        out_specs=P(None, ("beam", "freq"), "tm"),
        check_vma=False,
    )
```

```python
import functools

import jax
import jax.numpy as jnp
from jax import lax
from jax.experimental import pallas as pl
from jax.experimental.pallas import tpu as pltpu
from jax.sharding import PartitionSpec as P

LANES = 128
SUB = 8
TAPS = 128
VMEM = pltpu.MemorySpace.VMEM
SMEM = pltpu.MemorySpace.SMEM


def cdiv(a, b):
    return -(-a // b)


def round_up(a, b):
    return cdiv(a, b) * b


def shifted(src, start, width, shift, reach, lane):
    if reach >= LANES:
        start = start + shift // LANES
        shift = shift % LANES
    low = src[pl.ds(start, width), :]
    high = src[pl.ds(start + 1, width), :]
    return pltpu.roll(jnp.where(lane < shift, high, low), (LANES - shift) % LANES, 1)


def local_tree_kernel(levels, blocks, lead_blocks, own, pitch, spectra, lead, shifts, *refs):
    *outs, buf_a, buf_b = refs
    rows = spectra.shape[0]
    groups = len(outs)
    per = own // groups
    lane = lax.broadcasted_iota(jnp.int32, (pitch, LANES), 1)
    out_lane = lax.broadcasted_iota(jnp.int32, (blocks, LANES), 1)

    def spread(group, carry):
        at = pl.ds(pl.multiple_of(group * SUB, SUB), SUB)
        for b in range(blocks + lead_blocks):
            if b < blocks:
                v = spectra[at, b * LANES : (b + 1) * LANES]
            else:
                v = lead[at, (b - blocks) * LANES : (b - blocks + 1) * LANES]
            buf_a[pl.ds(group * (SUB * pitch) + b, SUB, stride=pitch), :] = v
        return carry

    lax.fori_loop(0, rows // SUB, spread, 0)

    src, dst = buf_a, buf_b
    for level in range(levels - 1):
        half = 2**level
        unroll = 4

        def pairs(n, carry, src=src, dst=dst, half=half, level=level):
            for u in range(unroll):
                p = n * unroll + u
                row_a = (p // half) * (2 * half) + p % half
                at_a = pl.multiple_of(row_a * pitch, SUB)
                at_b = pl.multiple_of((row_a + half) * pitch, SUB)
                a = src[pl.ds(at_a, pitch), :]
                for e, at in enumerate((at_a, at_b)):
                    shift = shifts[level * rows + row_a + e * half]
                    dst[pl.ds(at, pitch), :] = a + shifted(src, at_b, pitch, shift, half, lane)
            return carry

        lax.fori_loop(0, rows // 2 // unroll, pairs, 0)
        src, dst = dst, src

    level = levels - 1
    half = 2**level
    for group, out in enumerate(outs):
        unroll = 4

        def last_pairs(n, carry, src=src, out=out, group=group):
            for u in range(unroll):
                m = n * unroll + u
                row_a = (m // per) * own + group * per + m % per
                at_a = pl.multiple_of(row_a * pitch, SUB)
                at_b = pl.multiple_of((row_a + half) * pitch, SUB)
                a = src[pl.ds(at_a, blocks), :]
                for e in range(2):
                    row = row_a + e * half
                    shift = shifts[level * rows + row]
                    at = ((row // own) * per + m % per) * blocks
                    out[pl.ds(at, blocks), :] = a + shifted(src, at_b, blocks, shift, half, out_lane)
            return carry

        lax.fori_loop(0, rows // 2 // groups // unroll, last_pairs, 0)


def local_tree(spectra, lead, shifts, parts, groups):
    rows, span = spectra.shape
    levels = rows.bit_length() - 1
    blocks = span // LANES
    lead_blocks = lead.shape[1] // LANES
    own = rows // parts
    pitch = round_up(blocks + lead_blocks, SUB)
    spec = pl.BlockSpec(memory_space=VMEM)
    buf = pltpu.VMEM((rows * pitch + SUB, LANES), jnp.float32)
    shape = jax.ShapeDtypeStruct((rows // groups * blocks, LANES), jnp.float32)
    return pl.pallas_call(
        functools.partial(local_tree_kernel, levels, blocks, lead_blocks, own, pitch),
        out_shape=[shape] * groups,
        in_specs=[spec, spec, pl.BlockSpec(memory_space=SMEM)],
        out_specs=[spec] * groups,
        scratch_shapes=[buf, buf],
    )(spectra, lead, shifts)


def cross_kernel(bits, rows, own, first, blocks, halves, pitch, first_level, shifts, arrived, out, buf_a, buf_b):
    total = blocks * halves
    bands = 2**bits
    out_blocks = blocks + 1
    lane = lax.broadcasted_iota(jnp.int32, (total, LANES), 1)
    out_lane = lax.broadcasted_iota(jnp.int32, (out_blocks, LANES), 1)
    zero = jnp.zeros((pitch - total, LANES), jnp.float32)

    def gather(i, carry):
        for s in range(bands):
            at = (s * rows + i) * pitch
            for c in range(halves):
                piece = arrived[pl.ds(((s * halves + c) * rows + i) * blocks, blocks), :]
                buf_a[pl.ds(at + c * blocks, blocks), :] = piece
            for buf in (buf_a, buf_b):
                buf[pl.ds(at + total, pitch - total), :] = zero
        return carry

    lax.fori_loop(0, rows, gather, 0)

    src, dst = buf_a, buf_b
    for level in range(bits):
        step = 2**level
        reach = 2 ** (first_level + level)

        def one_row(i, carry, src=src, dst=dst, step=step, level=level, reach=reach):
            for j in range(bands):
                base = (j // (2 * step)) * (2 * step) + j % step
                shift = shifts[(level * bands + j) * own + first + i]
                at_a = pl.multiple_of((base * rows + i) * pitch, SUB)
                at_b = pl.multiple_of(((base + step) * rows + i) * pitch, SUB)
                if level < bits - 1:
                    a = src[pl.ds(at_a, total), :]
                    at = pl.multiple_of((j * rows + i) * pitch, SUB)
                    dst[pl.ds(at, total), :] = a + shifted(src, at_b, total, shift, reach, lane)
                    continue
                for c in range(halves):
                    a = src[pl.ds(at_a + c * blocks, out_blocks), :]
                    moved = shifted(src, at_b + c * blocks, out_blocks, shift, reach, out_lane)
                    out[pl.ds(((j * halves + c) * rows + i) * out_blocks, out_blocks), :] = a + moved
            return carry

        lax.fori_loop(0, rows, one_row, 0)
        src, dst = dst, src


def cross_tree(arrived, shifts, bits, own, group, groups, blocks, halves, first_level):
    bands = 2**bits
    reach = 2 ** (first_level + bits - 1)
    pitch = round_up(blocks * halves + cdiv(reach, LANES) + 2, SUB)
    rows = own // groups
    buf = pltpu.VMEM((bands * rows * pitch + SUB, LANES), jnp.float32)
    out_rows = bands * halves * (blocks + 1) * rows
    return pl.pallas_call(
        functools.partial(
            cross_kernel, bits, rows, own, group * rows, blocks, halves, pitch, first_level
        ),
        out_shape=jax.ShapeDtypeStruct((out_rows, LANES), jnp.float32),
        in_specs=[pl.BlockSpec(memory_space=SMEM), pl.BlockSpec(memory_space=VMEM)],
        out_specs=pl.BlockSpec(memory_space=VMEM),
        scratch_shapes=[buf, buf],
        cost_estimate=pl.CostEstimate(flops=0, bytes_accessed=20 * out_rows * LANES, transcendentals=0),
    )(shifts, arrived)


def filter_kernel(per_step, blocks, filters, widths, scaling, x, *refs):
    out, matrix = refs[-2:]
    rows = out.shape[1] * out.shape[2]

    @pl.when(pl.program_id(0) == 0)
    def _():
        pos = lax.broadcasted_iota(jnp.int32, (2 * TAPS, TAPS), 0)
        dist = pos - lax.broadcasted_iota(jnp.int32, (2 * TAPS, TAPS), 1)
        for w in range(filters):
            box = (dist >= 0) & (dist < widths[w])
            value = jnp.where(box, 1.0, 0.0).astype(jnp.bfloat16)
            for n in range(2):
                matrix[n * 2 * TAPS : (n + 1) * 2 * TAPS, w * TAPS : (w + 1) * TAPS] = value

    first = pl.program_id(0) * per_step
    pieces = [x[pl.ds(first + n, rows, stride=blocks + 1), :] for n in range(per_step + 1)]
    heads = [v.astype(jnp.bfloat16) for v in pieces]
    tails = [(v - h.astype(jnp.float32)).astype(jnp.bfloat16) for v, h in zip(pieces, heads)]
    together = 2 if filters % 2 == 0 else 1
    for k in range(per_step):
        lhs = jnp.concatenate([heads[k], heads[k + 1], tails[k], tails[k + 1]], axis=1)
        for w in range(0, filters, together):
            m = matrix[:, w * TAPS : (w + together) * TAPS]
            y = jnp.dot(lhs, m, preferred_element_type=jnp.float32)
            for n in range(together):
                part = y[:, n * TAPS : (n + 1) * TAPS] * scaling[w + n]
                out[w + n, :, :, k * LANES : (k + 1) * LANES] = part.reshape(out.shape[1], out.shape[2], LANES)


def filter_rows(x, into, widths, scaling, parts, own, group, groups, blocks):
    filters = widths.shape[0]
    per_step = 2 if blocks % 2 == 0 else 1
    rows = own // groups
    if rows % SUB:
        view, block, where = (filters, 1, parts * own), (filters, 1, parts * own), (0, 0, 0)
    else:
        view, block, where = (filters, parts, own), (filters, parts, rows), (0, 0, group)
    specs = [
        pl.BlockSpec(memory_space=SMEM),
        pl.BlockSpec(memory_space=SMEM),
        pl.BlockSpec(memory_space=VMEM),
    ]
    args = [widths, scaling, x]
    if into is not None:
        specs.append(pl.BlockSpec(memory_space=pl.ANY))
        args.append(into)
    cells = filters * parts * rows * blocks * LANES
    return pl.pallas_call(
        functools.partial(filter_kernel, per_step, blocks, filters),
        grid=(blocks // per_step,),
        out_shape=jax.ShapeDtypeStruct(view + (blocks * LANES,), jnp.float32),
        in_specs=specs,
        out_specs=pl.BlockSpec(block + (per_step * LANES,), lambda s: where + (s,)),
        scratch_shapes=[pltpu.VMEM((4 * TAPS, filters * TAPS), jnp.bfloat16)],
        input_output_aliases={} if into is None else {3: 0},
        cost_estimate=pl.CostEstimate(flops=1024 * cells, bytes_accessed=4 * cells, transcendentals=0),
    )(*args)


GROUPS = 2


def local(spectra, delays, widths):
    rows, span = spectra.shape
    all_levels, all_rows = delays.shape
    levels = rows.bit_length() - 1
    bits = all_levels - levels
    bands, halves = lax.axis_size("freq"), lax.axis_size("tm")
    parts = bands * halves
    own = rows // parts
    groups = GROUPS if own % (SUB * GROUPS) == 0 else 1
    blocks = span // LANES
    lead_width = cdiv(rows - 1, LANES) * LANES
    position = lax.axis_index("freq")
    lead = lax.ppermute(spectra[:, :lead_width], "tm", [(k, k - 1) for k in range(1, halves)])
    own_shifts = lax.dynamic_slice_in_dim(delays[:levels], position * rows, rows, 1).reshape(-1)
    mine = (position * halves + lax.axis_index("tm")) * own
    shifts = lax.dynamic_slice_in_dim(delays[levels:].reshape(bits, bands, rows), mine, own, 2)
    shifts = shifts.reshape(-1)
    scaling = 1.0 / jnp.sqrt(widths.astype(jnp.float32) * all_rows)

    def turn(x):
        x = x.reshape(parts, -1, LANES)
        return lax.all_to_all(x, ("freq", "tm"), 0, 0, tiled=True).reshape(-1, LANES)

    sections = [turn(x) for x in local_tree(spectra, lead, own_shifts, parts, groups)]
    rows_done = [
        turn(cross_tree(x, shifts, bits, own, g, groups, blocks, halves, levels))
        for g, x in enumerate(sections)
    ]
    filtered = None
    for g, x in enumerate(rows_done):
        filtered = filter_rows(x, filtered, widths, scaling, parts, own, g, groups, blocks)
    return filtered.reshape(widths.shape[0], rows, span)


def solution(mesh):
    return jax.shard_map(
        local,
        mesh=mesh,
        in_specs=(P(("beam", "freq"), "tm"), P(), P()),
        out_specs=P(None, ("beam", "freq"), "tm"),
        check_vma=False,
    )
```

```python
import functools

import jax
import jax.numpy as jnp
from jax import lax
from jax.experimental import pallas as pl
from jax.experimental.pallas import tpu as pltpu
from jax.sharding import PartitionSpec as P

LANES = 128
SUB = 8
TAPS = 128
VMEM = pltpu.MemorySpace.VMEM
SMEM = pltpu.MemorySpace.SMEM


def cdiv(a, b):
    return -(-a // b)


def round_up(a, b):
    return cdiv(a, b) * b


def shifted(src, start, width, shift, reach, lane):
    if reach >= LANES:
        start = start + lax.shift_right_logical(shift, LANES.bit_length() - 1)
        shift = shift & (LANES - 1)
    low = src[pl.ds(start, width), :]
    high = src[pl.ds(start + 1, width), :]
    return pltpu.roll(jnp.where(lane < shift, high, low), LANES - shift, 1)


def local_tree_kernel(levels, blocks, lead_blocks, own, pitch, spectra, lead, shifts, *refs):
    *outs, buf_a, buf_b = refs
    rows = spectra.shape[0]
    groups = len(outs)
    per = own // groups
    per_bits, own_bits = per.bit_length() - 1, own.bit_length() - 1
    lane = lax.broadcasted_iota(jnp.int32, (pitch, LANES), 1)
    out_lane = lax.broadcasted_iota(jnp.int32, (blocks, LANES), 1)

    def spread(group, carry):
        at = pl.ds(pl.multiple_of(group * SUB, SUB), SUB)
        for b in range(blocks + lead_blocks):
            if b < blocks:
                v = spectra[at, b * LANES : (b + 1) * LANES]
            else:
                v = lead[at, (b - blocks) * LANES : (b - blocks + 1) * LANES]
            buf_a[pl.ds(group * (SUB * pitch) + b, SUB, stride=pitch), :] = v
        return carry

    lax.fori_loop(0, rows // SUB, spread, 0)

    src, dst = buf_a, buf_b
    for level in range(levels - 1):
        half = 2**level
        unroll = min(8, rows // 2)

        def pairs(n, carry, src=src, dst=dst, half=half, level=level):
            for u in range(unroll):
                p = n * unroll + u
                row_a = ((p >> level) << (level + 1)) + (p & (half - 1))
                at_a = pl.multiple_of(row_a * pitch, SUB)
                at_b = pl.multiple_of((row_a + half) * pitch, SUB)
                a = src[pl.ds(at_a, pitch), :]
                for e, at in enumerate((at_a, at_b)):
                    shift = shifts[level * rows + row_a + e * half]
                    dst[pl.ds(at, pitch), :] = a + shifted(src, at_b, pitch, shift, half, lane)
            return carry

        lax.fori_loop(0, rows // 2 // unroll, pairs, 0)
        src, dst = dst, src

    level = levels - 1
    half = 2**level
    for group, out in enumerate(outs):
        unroll = 8 if rows // 2 // groups % 8 == 0 else 1

        def last_pairs(n, carry, src=src, out=out, group=group):
            for u in range(unroll):
                m = n * unroll + u
                row_a = (m >> per_bits) * own + group * per + (m & (per - 1))
                at_a = pl.multiple_of(row_a * pitch, SUB)
                at_b = pl.multiple_of((row_a + half) * pitch, SUB)
                a = src[pl.ds(at_a, blocks), :]
                for e in range(2):
                    row = row_a + e * half
                    shift = shifts[level * rows + row]
                    at = ((row >> own_bits) * per + (m & (per - 1))) * blocks
                    out[pl.ds(at, blocks), :] = a + shifted(src, at_b, blocks, shift, half, out_lane)
            return carry

        lax.fori_loop(0, rows // 2 // groups // unroll, last_pairs, 0)


def local_tree(spectra, lead, shifts, parts, groups):
    rows, span = spectra.shape
    levels = rows.bit_length() - 1
    blocks = span // LANES
    lead_blocks = lead.shape[1] // LANES
    own = rows // parts
    pitch = round_up(blocks + lead_blocks, SUB)
    spec = pl.BlockSpec(memory_space=VMEM)
    buf = pltpu.VMEM((rows * pitch + SUB, LANES), jnp.float32)
    shape = jax.ShapeDtypeStruct((rows // groups * blocks, LANES), jnp.float32)
    return pl.pallas_call(
        functools.partial(local_tree_kernel, levels, blocks, lead_blocks, own, pitch),
        out_shape=[shape] * groups,
        in_specs=[spec, spec, pl.BlockSpec(memory_space=SMEM)],
        out_specs=[spec] * groups,
        scratch_shapes=[buf, buf],
    )(spectra, lead, shifts)


def cross_kernel(bits, rows, own, first, blocks, halves, pitch, first_level, shifts, arrived, out, buf_a, buf_b):
    total = blocks * halves
    bands = 2**bits
    out_blocks = blocks + 1
    lane = lax.broadcasted_iota(jnp.int32, (total, LANES), 1)
    out_lane = lax.broadcasted_iota(jnp.int32, (out_blocks, LANES), 1)
    zero = jnp.zeros((pitch - total, LANES), jnp.float32)

    def gather(i, carry):
        for s in range(bands):
            at = (s * rows + i) * pitch
            for c in range(halves):
                piece = arrived[pl.ds(((s * halves + c) * rows + i) * blocks, blocks), :]
                buf_a[pl.ds(at + c * blocks, blocks), :] = piece
            for buf in (buf_a, buf_b):
                buf[pl.ds(at + total, pitch - total), :] = zero
        return carry

    lax.fori_loop(0, rows, gather, 0)

    src, dst = buf_a, buf_b
    for level in range(bits):
        step = 2**level
        reach = 2 ** (first_level + level)

        def one_row(i, carry, src=src, dst=dst, step=step, level=level, reach=reach):
            for j in range(bands):
                base = (j // (2 * step)) * (2 * step) + j % step
                shift = shifts[(level * bands + j) * own + first + i]
                at_a = pl.multiple_of((base * rows + i) * pitch, SUB)
                at_b = pl.multiple_of(((base + step) * rows + i) * pitch, SUB)
                if level < bits - 1:
                    a = src[pl.ds(at_a, total), :]
                    at = pl.multiple_of((j * rows + i) * pitch, SUB)
                    dst[pl.ds(at, total), :] = a + shifted(src, at_b, total, shift, reach, lane)
                    continue
                for c in range(halves):
                    a = src[pl.ds(at_a + c * blocks, out_blocks), :]
                    moved = shifted(src, at_b + c * blocks, out_blocks, shift, reach, out_lane)
                    out[pl.ds(((j * halves + c) * rows + i) * out_blocks, out_blocks), :] = a + moved
            return carry

        lax.fori_loop(0, rows, one_row, 0)
        src, dst = dst, src


def cross_tree(arrived, shifts, bits, own, group, groups, blocks, halves, first_level):
    bands = 2**bits
    reach = 2 ** (first_level + bits - 1)
    pitch = round_up(blocks * halves + cdiv(reach, LANES) + 2, SUB)
    rows = own // groups
    buf = pltpu.VMEM((bands * rows * pitch + SUB, LANES), jnp.float32)
    out_rows = bands * halves * (blocks + 1) * rows
    return pl.pallas_call(
        functools.partial(
            cross_kernel, bits, rows, own, group * rows, blocks, halves, pitch, first_level
        ),
        out_shape=jax.ShapeDtypeStruct((out_rows, LANES), jnp.float32),
        in_specs=[pl.BlockSpec(memory_space=SMEM), pl.BlockSpec(memory_space=VMEM)],
        out_specs=pl.BlockSpec(memory_space=VMEM),
        scratch_shapes=[buf, buf],
        cost_estimate=pl.CostEstimate(flops=0, bytes_accessed=20 * out_rows * LANES, transcendentals=0),
    )(shifts, arrived)


def filter_kernel(per_step, blocks, filters, widths, scaling, x, *refs):
    out, matrix = refs[-2:]
    rows = out.shape[1] * out.shape[2]

    @pl.when(pl.program_id(0) == 0)
    def _():
        pos = lax.broadcasted_iota(jnp.int32, (2 * TAPS, TAPS), 0)
        dist = pos - lax.broadcasted_iota(jnp.int32, (2 * TAPS, TAPS), 1)
        for w in range(filters):
            box = (dist >= 0) & (dist < widths[w])
            value = jnp.where(box, 1.0, 0.0).astype(jnp.bfloat16)
            for n in range(2):
                matrix[n * 2 * TAPS : (n + 1) * 2 * TAPS, w * TAPS : (w + 1) * TAPS] = value

    first = pl.program_id(0) * per_step
    pieces = [x[pl.ds(first + n, rows, stride=blocks + 1), :] for n in range(per_step + 1)]
    heads = [v.astype(jnp.bfloat16) for v in pieces]
    tails = [(v - h.astype(jnp.float32)).astype(jnp.bfloat16) for v, h in zip(pieces, heads)]
    together = 2 if filters % 2 == 0 else 1
    for k in range(per_step):
        lhs = jnp.concatenate([heads[k], heads[k + 1], tails[k], tails[k + 1]], axis=1)
        for w in range(0, filters, together):
            m = matrix[:, w * TAPS : (w + together) * TAPS]
            y = jnp.dot(lhs, m, preferred_element_type=jnp.float32)
            for n in range(together):
                part = y[:, n * TAPS : (n + 1) * TAPS] * scaling[w + n]
                out[w + n, :, :, k * LANES : (k + 1) * LANES] = part.reshape(out.shape[1], out.shape[2], LANES)


def filter_rows(x, into, widths, scaling, parts, own, group, groups, blocks):
    filters = widths.shape[0]
    per_step = 2 if blocks % 2 == 0 else 1
    rows = own // groups
    if rows % SUB:
        view, block, where = (filters, 1, parts * own), (filters, 1, parts * own), (0, 0, 0)
    else:
        view, block, where = (filters, parts, own), (filters, parts, rows), (0, 0, group)
    specs = [
        pl.BlockSpec(memory_space=SMEM),
        pl.BlockSpec(memory_space=SMEM),
        pl.BlockSpec(memory_space=VMEM),
    ]
    args = [widths, scaling, x]
    if into is not None:
        specs.append(pl.BlockSpec(memory_space=pl.ANY))
        args.append(into)
    cells = filters * parts * rows * blocks * LANES
    return pl.pallas_call(
        functools.partial(filter_kernel, per_step, blocks, filters),
        grid=(blocks // per_step,),
        out_shape=jax.ShapeDtypeStruct(view + (blocks * LANES,), jnp.float32),
        in_specs=specs,
        out_specs=pl.BlockSpec(block + (per_step * LANES,), lambda s: where + (s,)),
        scratch_shapes=[pltpu.VMEM((4 * TAPS, filters * TAPS), jnp.bfloat16)],
        input_output_aliases={} if into is None else {3: 0},
        cost_estimate=pl.CostEstimate(flops=1024 * cells, bytes_accessed=4 * cells, transcendentals=0),
    )(*args)


GROUPS = 2


def local(spectra, delays, widths):
    rows, span = spectra.shape
    all_levels, all_rows = delays.shape
    levels = rows.bit_length() - 1
    bits = all_levels - levels
    bands, halves = lax.axis_size("freq"), lax.axis_size("tm")
    parts = bands * halves
    own = rows // parts
    groups = GROUPS if own % (SUB * GROUPS) == 0 else 1
    blocks = span // LANES
    lead_width = cdiv(rows - 1, LANES) * LANES
    position = lax.axis_index("freq")
    lead = lax.ppermute(spectra[:, :lead_width], "tm", [(k, k - 1) for k in range(1, halves)])
    own_shifts = lax.dynamic_slice_in_dim(delays[:levels], position * rows, rows, 1).reshape(-1)
    mine = (position * halves + lax.axis_index("tm")) * own
    shifts = lax.dynamic_slice_in_dim(delays[levels:].reshape(bits, bands, rows), mine, own, 2)
    shifts = shifts.reshape(-1)
    scaling = 1.0 / jnp.sqrt(widths.astype(jnp.float32) * all_rows)

    def turn(x):
        x = x.reshape(parts, -1, LANES)
        return lax.all_to_all(x, ("freq", "tm"), 0, 0, tiled=True).reshape(-1, LANES)

    sections = [turn(x) for x in local_tree(spectra, lead, own_shifts, parts, groups)]
    rows_done = [
        turn(cross_tree(x, shifts, bits, own, g, groups, blocks, halves, levels))
        for g, x in enumerate(sections)
    ]
    filtered = None
    for g, x in enumerate(rows_done):
        filtered = filter_rows(x, filtered, widths, scaling, parts, own, g, groups, blocks)
    return filtered.reshape(widths.shape[0], rows, span)


def solution(mesh):
    return jax.shard_map(
        local,
        mesh=mesh,
        in_specs=(P(("beam", "freq"), "tm"), P(), P()),
        out_specs=P(None, ("beam", "freq"), "tm"),
        check_vma=False,
    )
```

```python
import functools

import jax
import jax.numpy as jnp
from jax import lax
from jax.experimental import pallas as pl
from jax.experimental.pallas import tpu as pltpu
from jax.sharding import PartitionSpec as P

LANES = 128
SUB = 8
TAPS = 128
VMEM = pltpu.MemorySpace.VMEM
SMEM = pltpu.MemorySpace.SMEM


def cdiv(a, b):
    return -(-a // b)


def round_up(a, b):
    return cdiv(a, b) * b


def shifted(src, start, width, shift, reach, lane):
    if reach >= LANES:
        start = start + lax.shift_right_logical(shift, LANES.bit_length() - 1)
        shift = shift & (LANES - 1)
    low = src[pl.ds(start, width), :]
    high = src[pl.ds(start + 1, width), :]
    return pltpu.roll(jnp.where(lane < shift, high, low), LANES - shift, 1)


def local_tree_kernel(levels, blocks, lead_blocks, own, pitch, spectra, lead, shifts, *refs):
    *outs, buf_a, buf_b = refs
    rows = spectra.shape[0]
    groups = len(outs)
    per = own // groups
    per_bits, own_bits = per.bit_length() - 1, own.bit_length() - 1
    lane = lax.broadcasted_iota(jnp.int32, (pitch, LANES), 1)
    out_lane = lax.broadcasted_iota(jnp.int32, (blocks, LANES), 1)

    def spread(group, carry):
        at = pl.ds(pl.multiple_of(group * SUB, SUB), SUB)
        for b in range(blocks + lead_blocks):
            if b < blocks:
                v = spectra[at, b * LANES : (b + 1) * LANES]
            else:
                v = lead[at, (b - blocks) * LANES : (b - blocks + 1) * LANES]
            buf_a[pl.ds(group * (SUB * pitch) + b, SUB, stride=pitch), :] = v
        return carry

    lax.fori_loop(0, rows // SUB, spread, 0)

    src, dst = buf_a, buf_b
    for level in range(levels - 1):
        half = 2**level
        unroll = min(8, rows // 2)

        def pairs(n, carry, src=src, dst=dst, half=half, level=level):
            for u in range(unroll):
                p = n * unroll + u
                row_a = ((p >> level) << (level + 1)) + (p & (half - 1))
                at_a = pl.multiple_of(row_a * pitch, SUB)
                at_b = pl.multiple_of((row_a + half) * pitch, SUB)
                a = src[pl.ds(at_a, pitch), :]
                for e, at in enumerate((at_a, at_b)):
                    shift = shifts[level * rows + row_a + e * half]
                    dst[pl.ds(at, pitch), :] = a + shifted(src, at_b, pitch, shift, half, lane)
            return carry

        lax.fori_loop(0, rows // 2 // unroll, pairs, 0)
        src, dst = dst, src

    level = levels - 1
    half = 2**level
    for group, out in enumerate(outs):
        unroll = 8 if rows // 2 // groups % 8 == 0 else 1

        def last_pairs(n, carry, src=src, out=out, group=group):
            for u in range(unroll):
                m = n * unroll + u
                row_a = (m >> per_bits) * own + group * per + (m & (per - 1))
                at_a = pl.multiple_of(row_a * pitch, SUB)
                at_b = pl.multiple_of((row_a + half) * pitch, SUB)
                a = src[pl.ds(at_a, blocks), :]
                for e in range(2):
                    row = row_a + e * half
                    shift = shifts[level * rows + row]
                    at = ((row >> own_bits) * per + (m & (per - 1))) * blocks
                    out[pl.ds(at, blocks), :] = a + shifted(src, at_b, blocks, shift, half, out_lane)
            return carry

        lax.fori_loop(0, rows // 2 // groups // unroll, last_pairs, 0)


def local_tree(spectra, lead, shifts, parts, groups):
    rows, span = spectra.shape
    levels = rows.bit_length() - 1
    blocks = span // LANES
    lead_blocks = lead.shape[1] // LANES
    own = rows // parts
    pitch = round_up(blocks + lead_blocks, SUB)
    spec = pl.BlockSpec(memory_space=VMEM)
    buf = pltpu.VMEM((rows * pitch + SUB, LANES), jnp.float32)
    shape = jax.ShapeDtypeStruct((rows // groups * blocks, LANES), jnp.float32)
    return pl.pallas_call(
        functools.partial(local_tree_kernel, levels, blocks, lead_blocks, own, pitch),
        out_shape=[shape] * groups,
        in_specs=[spec, spec, pl.BlockSpec(memory_space=SMEM)],
        out_specs=[spec] * groups,
        scratch_shapes=[buf, buf],
    )(spectra, lead, shifts)


def turn_kernel(bits, rows, blocks, halves, pitch, first_level, groups, shifts, *refs):
    xs, outs = refs[:groups], refs[groups : 2 * groups]
    arrived, ready = refs[2 * groups : 3 * groups], refs[3 * groups : 4 * groups]
    buf_a, buf_b, sems, own_sems = refs[4 * groups :]
    own = rows * groups
    total = blocks * halves
    bands = 2**bits
    parts = bands * halves
    out_blocks = blocks + 1
    me = lax.axis_index("freq") * halves + lax.axis_index("tm")
    beam = lax.axis_index("beam")

    def device(k):
        other = (me + k) % parts
        return other, (beam, other // halves, other % halves)

    barrier = pltpu.get_barrier_semaphore()
    for k in range(1, parts):
        pl.semaphore_signal(
            barrier, inc=1, device_id=device(k)[1], device_id_type=pl.DeviceIdType.MESH
        )
    pl.semaphore_wait(barrier, parts - 1)

    def send(src, dst, turn):
        copies = []
        for k in range(1, parts):
            other, where = device(k)
            c = pltpu.make_async_remote_copy(
                src_ref=src.at[other],
                dst_ref=dst.at[me],
                send_sem=sems.at[0, turn, k],
                recv_sem=sems.at[1, turn, k],
                device_id=where,
                device_id_type=pl.DeviceIdType.MESH,
            )
            c.start()
            copies.append(c)
        c = pltpu.make_async_copy(src.at[me], dst.at[me], own_sems.at[turn])
        c.start()
        copies.append(c)
        return copies

    def wait(copies):
        for c in copies:
            c.wait()

    first = [send(xs[g], arrived[g], g) for g in range(groups)]

    lane = lax.broadcasted_iota(jnp.int32, (total, LANES), 1)
    out_lane = lax.broadcasted_iota(jnp.int32, (out_blocks, LANES), 1)
    zero = jnp.zeros((pitch - total, LANES), jnp.float32)

    def clear(r, carry):
        for buf in (buf_a, buf_b):
            buf[pl.ds(r * pitch + total, pitch - total), :] = zero
        return carry

    lax.fori_loop(0, bands * rows, clear, 0)
    for buf in (buf_a, buf_b):
        buf[pl.ds(bands * rows * pitch, SUB), :] = jnp.zeros((SUB, LANES), jnp.float32)

    back = []
    for g in range(groups):
        wait(first[g])

        def gather(i, carry, g=g):
            for s in range(bands):
                at = (s * rows + i) * pitch
                for c in range(halves):
                    piece = arrived[g][s * halves + c, pl.ds(i * blocks, blocks), :]
                    buf_a[pl.ds(at + c * blocks, blocks), :] = piece
            return carry

        lax.fori_loop(0, rows, gather, 0)

        src, dst = buf_a, buf_b
        for level in range(bits):
            step = 2**level
            reach = 2 ** (first_level + level)

            def one_row(i, carry, src=src, dst=dst, step=step, level=level, reach=reach, g=g):
                for j in range(bands):
                    base = (j // (2 * step)) * (2 * step) + j % step
                    shift = shifts[(level * bands + j) * own + g * rows + i]
                    at_a = pl.multiple_of((base * rows + i) * pitch, SUB)
                    at_b = pl.multiple_of(((base + step) * rows + i) * pitch, SUB)
                    if level < bits - 1:
                        a = src[pl.ds(at_a, total), :]
                        at = pl.multiple_of((j * rows + i) * pitch, SUB)
                        dst[pl.ds(at, total), :] = a + shifted(src, at_b, total, shift, reach, lane)
                        continue
                    for c in range(halves):
                        a = src[pl.ds(at_a + c * blocks, out_blocks), :]
                        moved = shifted(src, at_b + c * blocks, out_blocks, shift, reach, out_lane)
                        ready[g][j * halves + c, pl.ds(i * out_blocks, out_blocks), :] = a + moved
                return carry

            lax.fori_loop(0, rows, one_row, 0)
            src, dst = dst, src
        back.append(send(ready[g], outs[g], groups + g))
    for copies in back:
        wait(copies)


def turn_and_cross(sections, shifts, bits, own, blocks, halves, first_level):
    groups = len(sections)
    bands = 2**bits
    parts = bands * halves
    reach = 2 ** (first_level + bits - 1)
    pitch = round_up(blocks * halves + cdiv(reach, LANES) + 2, SUB)
    rows = own // groups
    buf = pltpu.VMEM((bands * rows * pitch + SUB, LANES), jnp.float32)
    here = pl.BlockSpec(memory_space=pl.ANY)
    out_shape = jax.ShapeDtypeStruct((parts, rows * (blocks + 1), LANES), jnp.float32)
    return pl.pallas_call(
        functools.partial(turn_kernel, bits, rows, blocks, halves, pitch, first_level, groups),
        out_shape=[out_shape] * groups,
        in_specs=[pl.BlockSpec(memory_space=SMEM)] + [here] * groups,
        out_specs=[here] * groups,
        scratch_shapes=[pltpu.VMEM((parts, rows * blocks, LANES), jnp.float32)] * groups
        + [pltpu.VMEM((parts, rows * (blocks + 1), LANES), jnp.float32)] * groups
        + [buf, buf]
        + [
            pltpu.SemaphoreType.DMA((2, 2 * groups, parts)),
            pltpu.SemaphoreType.DMA((2 * groups,)),
        ],
        compiler_params=pltpu.CompilerParams(collective_id=0, has_side_effects=True),
    )(shifts, *sections)


def filter_kernel(per_step, blocks, filters, widths, scaling, x, *refs):
    out, matrix = refs[-2:]
    rows = out.shape[1] * out.shape[2]

    @pl.when(pl.program_id(0) == 0)
    def _():
        pos = lax.broadcasted_iota(jnp.int32, (2 * TAPS, TAPS), 0)
        dist = pos - lax.broadcasted_iota(jnp.int32, (2 * TAPS, TAPS), 1)
        for w in range(filters):
            box = (dist >= 0) & (dist < widths[w])
            value = jnp.where(box, 1.0, 0.0).astype(jnp.bfloat16)
            for n in range(2):
                matrix[n * 2 * TAPS : (n + 1) * 2 * TAPS, w * TAPS : (w + 1) * TAPS] = value

    first = pl.program_id(0) * per_step
    pieces = [x[pl.ds(first + n, rows, stride=blocks + 1), :] for n in range(per_step + 1)]
    heads = [v.astype(jnp.bfloat16) for v in pieces]
    tails = [(v - h.astype(jnp.float32)).astype(jnp.bfloat16) for v, h in zip(pieces, heads)]
    together = 2 if filters % 2 == 0 else 1
    for k in range(per_step):
        lhs = jnp.concatenate([heads[k], heads[k + 1], tails[k], tails[k + 1]], axis=1)
        for w in range(0, filters, together):
            m = matrix[:, w * TAPS : (w + together) * TAPS]
            y = jnp.dot(lhs, m, preferred_element_type=jnp.float32)
            for n in range(together):
                part = y[:, n * TAPS : (n + 1) * TAPS] * scaling[w + n]
                out[w + n, :, :, k * LANES : (k + 1) * LANES] = part.reshape(out.shape[1], out.shape[2], LANES)


def filter_rows(x, into, widths, scaling, parts, own, group, groups, blocks):
    filters = widths.shape[0]
    per_step = 2 if blocks % 2 == 0 else 1
    rows = own // groups
    if rows % SUB:
        view, block, where = (filters, 1, parts * own), (filters, 1, parts * own), (0, 0, 0)
    else:
        view, block, where = (filters, parts, own), (filters, parts, rows), (0, 0, group)
    specs = [
        pl.BlockSpec(memory_space=SMEM),
        pl.BlockSpec(memory_space=SMEM),
        pl.BlockSpec(memory_space=VMEM),
    ]
    args = [widths, scaling, x]
    if into is not None:
        specs.append(pl.BlockSpec(memory_space=pl.ANY))
        args.append(into)
    cells = filters * parts * rows * blocks * LANES
    return pl.pallas_call(
        functools.partial(filter_kernel, per_step, blocks, filters),
        grid=(blocks // per_step,),
        out_shape=jax.ShapeDtypeStruct(view + (blocks * LANES,), jnp.float32),
        in_specs=specs,
        out_specs=pl.BlockSpec(block + (per_step * LANES,), lambda s: where + (s,)),
        scratch_shapes=[pltpu.VMEM((4 * TAPS, filters * TAPS), jnp.bfloat16)],
        input_output_aliases={} if into is None else {3: 0},
        cost_estimate=pl.CostEstimate(flops=1024 * cells, bytes_accessed=4 * cells, transcendentals=0),
    )(*args)


GROUPS = 2


def local(spectra, delays, widths):
    rows, span = spectra.shape
    all_levels, all_rows = delays.shape
    levels = rows.bit_length() - 1
    bits = all_levels - levels
    bands, halves = lax.axis_size("freq"), lax.axis_size("tm")
    parts = bands * halves
    own = rows // parts
    groups = GROUPS if own % (SUB * GROUPS) == 0 else 1
    blocks = span // LANES
    lead_width = cdiv(rows - 1, LANES) * LANES
    position = lax.axis_index("freq")
    lead = lax.ppermute(spectra[:, :lead_width], "tm", [(k, k - 1) for k in range(1, halves)])
    own_shifts = lax.dynamic_slice_in_dim(delays[:levels], position * rows, rows, 1).reshape(-1)
    mine = (position * halves + lax.axis_index("tm")) * own
    shifts = lax.dynamic_slice_in_dim(delays[levels:].reshape(bits, bands, rows), mine, own, 2)
    shifts = shifts.reshape(-1)
    scaling = 1.0 / jnp.sqrt(widths.astype(jnp.float32) * all_rows)

    sections = local_tree(spectra, lead, own_shifts, parts, groups)
    sections = [x.reshape(parts, -1, LANES) for x in sections]
    rows_done = turn_and_cross(sections, shifts, bits, own, blocks, halves, levels)
    filtered = None
    for g, x in enumerate(rows_done):
        x = x.reshape(-1, LANES)
        filtered = filter_rows(x, filtered, widths, scaling, parts, own, g, groups, blocks)
    return filtered.reshape(widths.shape[0], rows, span)


def solution(mesh):
    return jax.shard_map(
        local,
        mesh=mesh,
        in_specs=(P(("beam", "freq"), "tm"), P(), P()),
        out_specs=P(None, ("beam", "freq"), "tm"),
        check_vma=False,
    )
```

```python
import functools

import jax
import jax.numpy as jnp
from jax import lax
from jax.experimental import pallas as pl
from jax.experimental.pallas import tpu as pltpu
from jax.sharding import PartitionSpec as P

LANES = 128
SUB = 8
TAPS = 128
VMEM = pltpu.MemorySpace.VMEM
SMEM = pltpu.MemorySpace.SMEM


def cdiv(a, b):
    return -(-a // b)


def round_up(a, b):
    return cdiv(a, b) * b


def shifted(src, start, width, shift, reach, lane):
    if reach >= LANES:
        start = start + lax.shift_right_logical(shift, LANES.bit_length() - 1)
        shift = shift & (LANES - 1)
    low = src[pl.ds(start, width), :]
    high = src[pl.ds(start + 1, width), :]
    return pltpu.roll(jnp.where(lane < shift, high, low), LANES - shift, 1)


def local_tree_kernel(levels, blocks, lead_blocks, own, pitch, spectra, lead, shifts, *refs):
    *outs, buf_a, buf_b = refs
    rows = spectra.shape[0]
    groups = len(outs)
    per = own // groups
    per_bits, own_bits = per.bit_length() - 1, own.bit_length() - 1
    lane = lax.broadcasted_iota(jnp.int32, (pitch, LANES), 1)
    out_lane = lax.broadcasted_iota(jnp.int32, (blocks, LANES), 1)

    def spread(group, carry):
        at = pl.ds(pl.multiple_of(group * SUB, SUB), SUB)
        for b in range(blocks + lead_blocks):
            if b < blocks:
                v = spectra[at, b * LANES : (b + 1) * LANES]
            else:
                v = lead[at, (b - blocks) * LANES : (b - blocks + 1) * LANES]
            buf_a[pl.ds(group * (SUB * pitch) + b, SUB, stride=pitch), :] = v
        return carry

    lax.fori_loop(0, rows // SUB, spread, 0)

    src, dst = buf_a, buf_b
    for level in range(levels - 1):
        half = 2**level
        unroll = min(8, rows // 2)

        def pairs(n, carry, src=src, dst=dst, half=half, level=level):
            for u in range(unroll):
                p = n * unroll + u
                row_a = ((p >> level) << (level + 1)) + (p & (half - 1))
                at_a = pl.multiple_of(row_a * pitch, SUB)
                at_b = pl.multiple_of((row_a + half) * pitch, SUB)
                a = src[pl.ds(at_a, pitch), :]
                for e, at in enumerate((at_a, at_b)):
                    shift = shifts[level * rows + row_a + e * half]
                    dst[pl.ds(at, pitch), :] = a + shifted(src, at_b, pitch, shift, half, lane)
            return carry

        lax.fori_loop(0, rows // 2 // unroll, pairs, 0)
        src, dst = dst, src

    level = levels - 1
    half = 2**level
    for group, out in enumerate(outs):
        unroll = 8 if rows // 2 // groups % 8 == 0 else 1

        def last_pairs(n, carry, src=src, out=out, group=group):
            for u in range(unroll):
                m = n * unroll + u
                row_a = (m >> per_bits) * own + group * per + (m & (per - 1))
                at_a = pl.multiple_of(row_a * pitch, SUB)
                at_b = pl.multiple_of((row_a + half) * pitch, SUB)
                a = src[pl.ds(at_a, blocks), :]
                for e in range(2):
                    row = row_a + e * half
                    shift = shifts[level * rows + row]
                    at = ((row >> own_bits) * per + (m & (per - 1))) * blocks
                    out[pl.ds(at, blocks), :] = a + shifted(src, at_b, blocks, shift, half, out_lane)
            return carry

        lax.fori_loop(0, rows // 2 // groups // unroll, last_pairs, 0)


def local_tree(spectra, lead, shifts, parts, groups):
    rows, span = spectra.shape
    levels = rows.bit_length() - 1
    blocks = span // LANES
    lead_blocks = lead.shape[1] // LANES
    own = rows // parts
    pitch = round_up(blocks + lead_blocks, SUB)
    spec = pl.BlockSpec(memory_space=VMEM)
    buf = pltpu.VMEM((rows * pitch + SUB, LANES), jnp.float32)
    shape = jax.ShapeDtypeStruct((rows // groups * blocks, LANES), jnp.float32)
    return pl.pallas_call(
        functools.partial(local_tree_kernel, levels, blocks, lead_blocks, own, pitch),
        out_shape=[shape] * groups,
        in_specs=[spec, spec, pl.BlockSpec(memory_space=SMEM)],
        out_specs=[spec] * groups,
        scratch_shapes=[buf, buf],
    )(spectra, lead, shifts)


def turn_kernel(bits, rows, blocks, halves, pitch, first_level, groups, shifts, *refs):
    xs, outs = refs[:groups], refs[groups : 2 * groups]
    arrived, ready = refs[2 * groups : 3 * groups], refs[3 * groups : 4 * groups]
    buf_a, buf_b, sems, own_sems = refs[4 * groups :]
    own = rows * groups
    total = blocks * halves
    bands = 2**bits
    parts = bands * halves
    out_blocks = blocks + 1
    me = lax.axis_index("freq") * halves + lax.axis_index("tm")
    beam = lax.axis_index("beam")

    def device(k):
        other = (me + k) % parts
        return other, (beam, other // halves, other % halves)

    barrier = pltpu.get_barrier_semaphore()
    for k in range(1, parts):
        pl.semaphore_signal(
            barrier, inc=1, device_id=device(k)[1], device_id_type=pl.DeviceIdType.MESH
        )
    pl.semaphore_wait(barrier, parts - 1)

    def send(src, dst, turn):
        copies = []
        for k in range(1, parts):
            other, where = device(k)
            c = pltpu.make_async_remote_copy(
                src_ref=src.at[other],
                dst_ref=dst.at[me],
                send_sem=sems.at[0, turn, k],
                recv_sem=sems.at[1, turn, k],
                device_id=where,
                device_id_type=pl.DeviceIdType.MESH,
            )
            c.start()
            copies.append(c)
        c = pltpu.make_async_copy(src.at[me], dst.at[me], own_sems.at[turn])
        c.start()
        copies.append(c)
        return copies

    def wait(copies):
        for c in copies:
            c.wait()

    first = [send(xs[g], arrived[g], g) for g in range(groups)]

    lane = lax.broadcasted_iota(jnp.int32, (total, LANES), 1)
    out_lane = lax.broadcasted_iota(jnp.int32, (out_blocks, LANES), 1)
    zero = jnp.zeros((pitch - total, LANES), jnp.float32)

    def clear(r, carry):
        for buf in (buf_a, buf_b):
            buf[pl.ds(r * pitch + total, pitch - total), :] = zero
        return carry

    lax.fori_loop(0, bands * rows, clear, 0)
    for buf in (buf_a, buf_b):
        buf[pl.ds(bands * rows * pitch, SUB), :] = jnp.zeros((SUB, LANES), jnp.float32)

    back = []
    for g in range(groups):
        wait(first[g])

        def gather(i, carry, g=g):
            for s in range(bands):
                at = (s * rows + i) * pitch
                for c in range(halves):
                    piece = arrived[g][s * halves + c, pl.ds(i * blocks, blocks), :]
                    buf_a[pl.ds(at + c * blocks, blocks), :] = piece
            return carry

        lax.fori_loop(0, rows, gather, 0)

        src, dst = buf_a, buf_b
        for level in range(bits):
            step = 2**level
            reach = 2 ** (first_level + level)

            def one_row(i, carry, src=src, dst=dst, step=step, level=level, reach=reach, g=g):
                for j in range(bands):
                    base = (j // (2 * step)) * (2 * step) + j % step
                    shift = shifts[(level * bands + j) * own + g * rows + i]
                    at_a = pl.multiple_of((base * rows + i) * pitch, SUB)
                    at_b = pl.multiple_of(((base + step) * rows + i) * pitch, SUB)
                    if level < bits - 1:
                        a = src[pl.ds(at_a, total), :]
                        at = pl.multiple_of((j * rows + i) * pitch, SUB)
                        dst[pl.ds(at, total), :] = a + shifted(src, at_b, total, shift, reach, lane)
                        continue
                    for c in range(halves):
                        a = src[pl.ds(at_a + c * blocks, out_blocks), :]
                        moved = shifted(src, at_b + c * blocks, out_blocks, shift, reach, out_lane)
                        ready[g][j * halves + c, pl.ds(i * out_blocks, out_blocks), :] = a + moved
                return carry

            lax.fori_loop(0, rows, one_row, 0)
            src, dst = dst, src
        back.append(send(ready[g], outs[g], groups + g))
    for copies in back:
        wait(copies)


def turn_and_cross(sections, shifts, bits, own, blocks, halves, first_level):
    groups = len(sections)
    bands = 2**bits
    parts = bands * halves
    reach = 2 ** (first_level + bits - 1)
    pitch = round_up(blocks * halves + cdiv(reach, LANES) + 2, SUB)
    rows = own // groups
    buf = pltpu.VMEM((bands * rows * pitch + SUB, LANES), jnp.float32)
    here = pl.BlockSpec(memory_space=pl.ANY)
    out_shape = jax.ShapeDtypeStruct((parts, rows * (blocks + 1), LANES), jnp.float32)
    return pl.pallas_call(
        functools.partial(turn_kernel, bits, rows, blocks, halves, pitch, first_level, groups),
        out_shape=[out_shape] * groups,
        in_specs=[pl.BlockSpec(memory_space=SMEM)] + [here] * groups,
        out_specs=[here] * groups,
        scratch_shapes=[pltpu.VMEM((parts, rows * blocks, LANES), jnp.float32)] * groups
        + [pltpu.VMEM((parts, rows * (blocks + 1), LANES), jnp.float32)] * groups
        + [buf, buf]
        + [
            pltpu.SemaphoreType.DMA((2, 2 * groups, parts)),
            pltpu.SemaphoreType.DMA((2 * groups,)),
        ],
        compiler_params=pltpu.CompilerParams(collective_id=0, has_side_effects=True),
    )(shifts, *sections)


def filter_kernel(per_step, blocks, filters, widths, scaling, x, *refs):
    out, matrix = refs[-2:]
    rows = out.shape[1] * out.shape[2]

    @pl.when(pl.program_id(0) == 0)
    def _():
        pos = lax.broadcasted_iota(jnp.int32, (2 * TAPS, TAPS), 0)
        dist = pos - lax.broadcasted_iota(jnp.int32, (2 * TAPS, TAPS), 1)
        for w in range(filters):
            box = (dist >= 0) & (dist < widths[w])
            value = jnp.where(box, 1.0, 0.0).astype(jnp.bfloat16)
            for n in range(2):
                matrix[n * 2 * TAPS : (n + 1) * 2 * TAPS, w * TAPS : (w + 1) * TAPS] = value

    first = pl.program_id(0) * per_step
    pieces = [x[pl.ds(first + n, rows, stride=blocks + 1), :] for n in range(per_step + 1)]
    heads = [v.astype(jnp.bfloat16) for v in pieces]
    tails = [(v - h.astype(jnp.float32)).astype(jnp.bfloat16) for v, h in zip(pieces, heads)]
    together = 2 if filters % 2 == 0 else 1
    for k in range(per_step):
        lhs = jnp.concatenate([heads[k], heads[k + 1], tails[k], tails[k + 1]], axis=1)
        for w in range(0, filters, together):
            m = matrix[:, w * TAPS : (w + together) * TAPS]
            y = jnp.dot(lhs, m, preferred_element_type=jnp.float32)
            for n in range(together):
                part = y[:, n * TAPS : (n + 1) * TAPS] * scaling[w + n]
                out[w + n, :, :, k * LANES : (k + 1) * LANES] = part.reshape(out.shape[1], out.shape[2], LANES)


def filter_rows(x, into, widths, scaling, parts, own, group, groups, blocks):
    filters = widths.shape[0]
    per_step = 4 if blocks % 4 == 0 else 1
    rows = own // groups
    if rows % SUB:
        view, block, where = (filters, 1, parts * own), (filters, 1, parts * own), (0, 0, 0)
    else:
        view, block, where = (filters, parts, own), (filters, parts, rows), (0, 0, group)
    specs = [
        pl.BlockSpec(memory_space=SMEM),
        pl.BlockSpec(memory_space=SMEM),
        pl.BlockSpec(memory_space=VMEM),
    ]
    args = [widths, scaling, x]
    if into is not None:
        specs.append(pl.BlockSpec(memory_space=pl.ANY))
        args.append(into)
    cells = filters * parts * rows * blocks * LANES
    return pl.pallas_call(
        functools.partial(filter_kernel, per_step, blocks, filters),
        grid=(blocks // per_step,),
        out_shape=jax.ShapeDtypeStruct(view + (blocks * LANES,), jnp.float32),
        in_specs=specs,
        out_specs=pl.BlockSpec(block + (per_step * LANES,), lambda s: where + (s,)),
        scratch_shapes=[pltpu.VMEM((4 * TAPS, filters * TAPS), jnp.bfloat16)],
        input_output_aliases={} if into is None else {3: 0},
        cost_estimate=pl.CostEstimate(flops=1024 * cells, bytes_accessed=4 * cells, transcendentals=0),
    )(*args)


GROUPS = 2


def local(spectra, delays, widths):
    rows, span = spectra.shape
    all_levels, all_rows = delays.shape
    levels = rows.bit_length() - 1
    bits = all_levels - levels
    bands, halves = lax.axis_size("freq"), lax.axis_size("tm")
    parts = bands * halves
    own = rows // parts
    groups = GROUPS if own % (SUB * GROUPS) == 0 else 1
    blocks = span // LANES
    lead_width = cdiv(rows - 1, LANES) * LANES
    position = lax.axis_index("freq")
    lead = lax.ppermute(spectra[:, :lead_width], "tm", [(k, k - 1) for k in range(1, halves)])
    own_shifts = lax.dynamic_slice_in_dim(delays[:levels], position * rows, rows, 1).reshape(-1)
    mine = (position * halves + lax.axis_index("tm")) * own
    shifts = lax.dynamic_slice_in_dim(delays[levels:].reshape(bits, bands, rows), mine, own, 2)
    shifts = shifts.reshape(-1)
    scaling = 1.0 / jnp.sqrt(widths.astype(jnp.float32) * all_rows)

    sections = local_tree(spectra, lead, own_shifts, parts, groups)
    sections = [x.reshape(parts, -1, LANES) for x in sections]
    rows_done = turn_and_cross(sections, shifts, bits, own, blocks, halves, levels)
    filtered = None
    for g, x in enumerate(rows_done):
        x = x.reshape(-1, LANES)
        filtered = filter_rows(x, filtered, widths, scaling, parts, own, g, groups, blocks)
    return filtered.reshape(widths.shape[0], rows, span)


def solution(mesh):
    return jax.shard_map(
        local,
        mesh=mesh,
        in_specs=(P(("beam", "freq"), "tm"), P(), P()),
        out_specs=P(None, ("beam", "freq"), "tm"),
        check_vma=False,
    )
```
